256 devices in a mesh: leaf: 16 (over z, core), group: 16 (over x, y).
Axes of the slice: x: 4, y: 4, z: 8, core: 2. Of those that a mesh axis runs over, the one named last changes fastest.
Arguments:
- tile_fields: bfloat16 [2048, 32, 32, 512], P(('leaf', 'group')), may hold values from -2500 to 2500
- routes: int32 [256, 8], P(('leaf', 'group')), may hold values from 0 to 15, as said below
- counts: int32 [256], P(('leaf', 'group')), may hold values from 5 to 8
Outputs:
- factor: float32 [16, 16], replicated
- mode_blocks: float32 [4096, 256, 256], P(('leaf', 'group'))
The draws below stay inside these ranges and needn't reach their ends.
Inputs may be any that keep to these rules, and one draw needn't show every extreme that they name: `routes`: the 8 entries of a device are distinct. In every group some leaf index is named by an occupied slot of every device of the group, and every leaf index is named by an occupied slot of some device of the group.
All inputs are finite; a program needn't handle non-finite values.
Results may differ from the reference program's by a relative error of at most 0.012.
The reference program's roundings to bfloat16 on the way (of `smoother`, `first_pass`, `second_pass` and `filtered`) count: a program that leaves them out, or rounds other values in their place, can miss the bound.
Values may be sent and summed in bfloat16 or wider, within the bound.
A program may use at most 128 MiB of HBM per device.

```python
import math
import jax
import jax.numpy as jnp
from jax import lax

TILE = 32
SUB = 16
K = 16
SLOTS = 8
ROWS_ALL = 8388608
N_LEAF = 16
N_GROUP = 16


def draw_tile_fields(key, part):
    devices_all = N_LEAF * N_GROUP
    row_count = devices_all * SLOTS
    key_common, key_noise, key_amp, key_cols = jax.random.split(key, 4)
    common = jnp.clip(jax.random.normal(key_common, (row_count, TILE, TILE, TILE, 1), jnp.float32), -4.0, 4.0)
    noise_part = jnp.clip(jax.random.normal(key_noise, (row_count, TILE, TILE, TILE, K), jnp.float32), -4.0, 4.0)
    amplitude = jnp.exp(jax.random.uniform(key_amp, (row_count,), jnp.float32, 0.0, math.log(10.0)))
    columns = jnp.exp(jax.random.uniform(key_cols, (K,), jnp.float32, 0.0, math.log(10.0)))
    owner_index = (jnp.arange(row_count) // SLOTS).astype(jnp.float32)
    rise_factor = 1.0 + 2.0 * owner_index / max(devices_all - 1, 1)
    scale_rows = amplitude * rise_factor
    values = scale_rows[:, None, None, None, None] * columns * (common + noise_part)
    return values.reshape(row_count, TILE, TILE, TILE * K).astype(jnp.bfloat16)


def route_plan(key):
    devices_all = N_LEAF * N_GROUP
    key_count, key_hub, key_shift, key_perm = jax.random.split(jax.random.fold_in(key, 7), 4)
    counts = jax.random.randint(key_count, (devices_all,), SLOTS // 2 + 1, SLOTS + 1).astype(jnp.int32)
    counts = counts.at[0].set(SLOTS).at[1].set(SLOTS // 2 + 1)
    hub_leaf = jax.random.randint(key_hub, (N_GROUP,), 0, N_LEAF)
    shift_leaf = jax.random.randint(key_shift, (N_GROUP,), 0, N_LEAF)
    device_index = jnp.arange(devices_all)
    leaf_index = device_index // N_GROUP
    group_index = device_index % N_GROUP
    second_leaf = (leaf_index + shift_leaf[group_index]) % N_LEAF
    perm_keys = jax.random.split(key_perm, devices_all)
    random_rank = jax.vmap(lambda one_key: jax.random.permutation(one_key, N_LEAF))(perm_keys)
    dest_index = jnp.arange(N_LEAF)[None, :]
    scores = random_rank + N_LEAF * (dest_index == second_leaf[:, None]).astype(jnp.int32)
    scores = scores + 2 * N_LEAF * (dest_index == hub_leaf[group_index][:, None]).astype(jnp.int32)
    ordering = jnp.argsort(-scores, axis=1, stable=True)[:, :SLOTS]
    return (ordering.astype(jnp.int32), counts)


def draw_routes(key, part):
    return route_plan(key)[0]


def draw_counts(key, part):
    return route_plan(key)[1]


def setup_inputs(seed: int = 0) -> dict:
    seeds = jax.random.split(jax.random.key(seed), 4)
    tile_fields = draw_tile_fields(jax.random.fold_in(seeds[3], 71), 0)
    routes = draw_routes(jax.random.fold_in(seeds[3], 71), 0)
    counts = draw_counts(jax.random.fold_in(seeds[3], 71), 0)
    return {"tile_fields": tile_fields, "routes": routes, "counts": counts}


def smoother(length):
    half_edge = length // 2
    row_index = jnp.arange(half_edge)[:, None]
    col_index = jnp.arange(length)[None, :]
    offset = (col_index - 2 * row_index).astype(jnp.float32)
    tap_offsets = jnp.arange(-4, 5).astype(jnp.float32)
    normalizer = jnp.sum(jnp.exp(-tap_offsets * tap_offsets / 4.5))
    weights = jnp.where(jnp.abs(offset) <= 4.0, jnp.exp(-offset * offset / 4.5) / normalizer, 0.0)
    return weights.astype(jnp.bfloat16)

def cholesky_upper(gram):
    order = gram.shape[0]
    positions = jnp.arange(order)
    upper = jnp.zeros_like(gram)
    for row_index in range(order):
        partial_row = gram[row_index] - lax.optimization_barrier(jnp.sum(upper[:, row_index][:, None] * upper, axis=0))
        pivot = jnp.sqrt(partial_row[row_index])
        new_row = jnp.where(positions >= row_index, partial_row / pivot, jnp.zeros_like(partial_row))
        upper = upper.at[row_index].set(new_row)
    return upper

def invert_upper(upper):
    order = upper.shape[0]
    positions = jnp.arange(order)
    identity = jnp.eye(order, dtype=upper.dtype)
    result = jnp.zeros_like(upper)
    for row_index in range(order - 1, -1, -1):
        off_diagonal = jnp.where(positions > row_index, upper[row_index], jnp.zeros_like(upper[row_index]))
        partial_row = identity[row_index] - lax.optimization_barrier(jnp.sum(off_diagonal[:, None] * result, axis=0))
        result = result.at[row_index].set(partial_row / upper[row_index, row_index])
    return result

def filter_one(tile_piece):
    weights = smoother(TILE).astype(jnp.float32)
    highest = lax.Precision.HIGHEST
    first_pass = jnp.einsum('ix,xr->ir', weights, tile_piece.reshape(TILE, TILE * TILE * K).astype(jnp.float32), precision=highest).astype(jnp.bfloat16)
    second_pass = jnp.einsum('jy,iyc->ijc', weights, first_pass.reshape(SUB, TILE, TILE * K).astype(jnp.float32), precision=highest).astype(jnp.bfloat16)
    third_pass = jnp.einsum('lz,azk->alk', weights, second_pass.reshape(SUB * SUB, TILE, K).astype(jnp.float32), precision=highest).astype(jnp.bfloat16)
    return third_pass.reshape(SUB * SUB, SUB * K)

def reference(tile_fields, routes, counts):
    highest = lax.Precision.HIGHEST
    devices_all = N_LEAF * N_GROUP
    filtered = lax.map(filter_one, tile_fields)
    valid_mask = jnp.arange(SLOTS)[None, :] < counts[:, None]
    keep_mask = valid_mask.astype(jnp.bfloat16)
    filtered = filtered.reshape(devices_all, SLOTS, SUB * SUB, SUB * K) * keep_mask[:, :, None, None]

    def add_gram(gram_total, device_block):
        flat_rows = device_block.reshape(-1, K).astype(jnp.float32)
        return (gram_total + jnp.dot(flat_rows.T, flat_rows, precision=highest), None)
    gram_total, _ = lax.scan(add_gram, jnp.zeros((K, K), jnp.float32), filtered)
    factor = cholesky_upper(gram_total / ROWS_ALL)
    inverse = invert_upper(factor)
    routed_hits = ((routes[:, :, None] == jnp.arange(N_LEAF)[None, None, :]) & valid_mask[:, :, None]).astype(jnp.float32)
    routed_hits = routed_hits.reshape(N_LEAF, N_GROUP, SLOTS, N_LEAF)
    source = filtered.reshape(N_LEAF, N_GROUP, SLOTS, SUB * SUB, SUB * K).astype(jnp.float32)

    def for_dest(dest_leaf):
        chosen = routed_hits[:, :, :, dest_leaf]
        placed = jnp.einsum('sgt,sgtab->gsab', chosen, source, precision=highest)
        flat_rows = placed.reshape(N_GROUP, N_LEAF, SUB * SUB, SUB, K)
        result = jnp.einsum('gsazk,kl->gsazl', flat_rows, inverse, precision=highest)
        return result.reshape(N_GROUP, N_LEAF, SUB * SUB, SUB * K)
    mode_blocks = lax.map(for_dest, jnp.arange(N_LEAF))
    return (factor, mode_blocks.reshape(N_LEAF * N_GROUP * N_LEAF, SUB * SUB, SUB * K))
```

```python
import functools

import jax
import jax.numpy as jnp
import ml_dtypes
import numpy as np
from jax import lax
from jax.experimental import pallas as pl
from jax.experimental.pallas import tpu as pltpu
from jax.sharding import PartitionSpec as P

MESH = pl.DeviceIdType.MESH
F32 = jnp.float32
BF16 = jnp.bfloat16


def smoother(length):
    half_edge = length // 2
    row_index = np.arange(half_edge)[:, None]
    col_index = np.arange(length)[None, :]
    offset = (col_index - 2 * row_index).astype(np.float32)
    tap_offsets = np.arange(-4, 5).astype(np.float32)
    normalizer = np.sum(np.exp(-tap_offsets * tap_offsets / np.float32(4.5)), dtype=np.float32)
    taps = np.exp(-offset * offset / np.float32(4.5)) / normalizer
    weights = np.where(np.abs(offset) <= 4.0, taps, np.float32(0.0))
    return weights.astype(ml_dtypes.bfloat16).astype(np.float32)


def filter_tables(edge, snapshots):
    weights = smoother(edge)
    half = edge // 2
    table_x = np.kron(weights, np.eye(half, dtype=np.float32))
    table_y = np.stack(
        [np.kron(np.eye(half, dtype=np.float32), weights[:, h * half : (h + 1) * half]) for h in range(2)]
    )
    table_z = np.kron(weights.T, np.eye(snapshots, dtype=np.float32))
    as_bf16 = lambda a: a.astype(ml_dtypes.bfloat16)
    return as_bf16(table_x), as_bf16(table_y), as_bf16(table_z)


def dot(a, b):
    return jnp.dot(a, b, preferred_element_type=F32)


def filter_tile(tile, table_x, table_y, table_z):
    edge = tile.shape[0]
    half = edge // 2
    width = tile.shape[2]
    second = None
    for h in range(2):
        rows = tile[:, h * half : (h + 1) * half, :].reshape(edge * half, width)
        first = dot(table_x[...], rows).astype(BF16)
        term = dot(table_y[h], first)
        second = term if second is None else second + term
    return dot(second.astype(BF16), table_z[...]).astype(BF16)


def fold_gram(gram, snapshots):
    size = gram.shape[0]
    rows = lax.broadcasted_iota(jnp.int32, gram.shape, 0) // snapshots
    cols = lax.broadcasted_iota(jnp.int32, gram.shape, 1) // snapshots
    kept = jnp.where(rows == cols, gram, 0.0)
    strip = jnp.sum(kept.reshape(size // snapshots, snapshots, size), axis=0)
    folded = strip[:, :128]
    for start in range(128, size, 128):
        folded = folded + strip[:, start : start + 128]
    shift = 64
    while shift >= snapshots:
        folded = folded + pltpu.roll(folded, shift, axis=1)
        shift //= 2
    return folded


def factor_and_inverse(gram):
    order = gram.shape[0]
    rows = lax.broadcasted_iota(jnp.int32, gram.shape, 0)
    cols = lax.rem(lax.broadcasted_iota(jnp.int32, gram.shape, 1), order)
    rest = gram
    upper = jnp.zeros_like(gram)
    columns = []
    pivots = []
    for r in range(order):
        pivot = jnp.sqrt(rest[r : r + 1, r : r + 1])
        row = jnp.where(cols[:1] >= r, rest[r : r + 1, :] / pivot, 0.0)
        column = jnp.where(rows[:, :1] >= r, rest[:, r : r + 1] / pivot, 0.0)
        upper = jnp.where(rows == r, row, upper)
        columns.append(column)
        pivots.append(pivot)
        rest = rest - column * row
    inverse = jnp.zeros_like(gram)
    for r in range(order - 1, -1, -1):
        beyond = jnp.where(rows[:, :1] > r, columns[r], 0.0)
        unit = jnp.where(cols[:1] == r, 1.0, 0.0)
        row = (unit - jnp.sum(beyond * inverse, axis=0, keepdims=True)) / pivots[r]
        inverse = jnp.where(rows == r, row, inverse)
    return upper, inverse


def all_sum(axis, peers, buffer, send_sems, recv_sems):
    me = lax.axis_index(axis)

    def copy_to(peer):
        return pltpu.make_async_remote_copy(
            src_ref=buffer.at[me],
            dst_ref=buffer.at[me],
            send_sem=send_sems.at[peer],
            recv_sem=recv_sems.at[me],
            device_id={axis: peer},
            device_id_type=MESH,
        )

    def copy_from(peer):
        return pltpu.make_async_remote_copy(
            src_ref=buffer.at[me],
            dst_ref=buffer.at[peer],
            send_sem=send_sems.at[peer],
            recv_sem=recv_sems.at[peer],
            device_id={axis: peer},
            device_id_type=MESH,
        )

    @pl.loop(1, peers)
    def _(step):
        copy_to(lax.rem(me + step, peers)).start()

    @pl.loop(1, peers)
    def _(step):
        copy_from(lax.rem(me + step, peers)).wait_recv()

    total = buffer[0]
    for p in range(1, peers):
        total = total + buffer[p]

    @pl.loop(1, peers)
    def _(step):
        copy_to(lax.rem(me + step, peers)).wait_send()

    return total


def exchange_kernel(
    leaves, groups, snapshots, rows_all, early,
    tiles, routes, counts, table_x, table_y, table_z,
    arrived, factor_out, inverse_out,
    local, outgoing, gram, group_buf, leaf_buf,
    load_sems, self_sem, send_sems, recv_sems, group_send, group_recv, leaf_send, leaf_recv,
):
    slots = tiles.shape[0]
    me = lax.axis_index("leaf")
    my_group = lax.axis_index("group")
    chips = leaves // 2

    def load(t):
        return pltpu.make_async_copy(tiles.at[t], local.at[t], load_sems.at[t])

    for t in range(slots):
        load(t).start()

    barrier = pltpu.get_barrier_semaphore()

    @pl.loop(1, leaves)
    def _(step):
        pl.semaphore_signal(
            barrier, inc=1, device_id={"leaf": lax.rem(me + step, leaves)}, device_id_type=MESH
        )

    @pl.loop(1, groups)
    def _(step):
        pl.semaphore_signal(
            barrier, inc=1, device_id={"group": lax.rem(my_group + step, groups)}, device_id_type=MESH
        )

    gram[...] = jnp.zeros_like(gram)
    for t in range(slots):
        load(t).wait()
    pl.semaphore_wait(barrier, leaves + groups - 2)

    def dest_of(k):
        j = k // 2
        turn = chips // 2 + jnp.where(lax.rem(j, 2) == 0, j // 2, -((j + 1) // 2))
        chip = lax.rem(me // 2 + turn, chips)
        core = lax.rem(lax.rem(me, 2) + lax.rem(k, 2) + 1, 2)
        return chip * 2 + core

    def copy_to(k):
        return pltpu.make_async_remote_copy(
            src_ref=outgoing.at[k],
            dst_ref=arrived.at[me],
            send_sem=send_sems.at[k],
            recv_sem=recv_sems.at[me],
            device_id={"leaf": dest_of(k)},
            device_id_type=MESH,
        )

    def copy_from(source):
        return pltpu.make_async_remote_copy(
            src_ref=outgoing.at[0],
            dst_ref=arrived.at[source],
            send_sem=send_sems.at[0],
            recv_sem=recv_sems.at[source],
            device_id={"leaf": source},
            device_id_type=MESH,
        )

    count = counts[0]

    def prepare(k):
        dest = dest_of(k)
        slot = jnp.int32(0)
        found = jnp.int32(0)
        for t in range(slots):
            hit = jnp.where((routes[0, t] == dest) & (t < count), 1, 0)
            slot = slot + hit * t
            found = found + hit
        block = filter_tile(local[slot], table_x, table_y, table_z)
        block = jnp.where(found > 0, block, jnp.zeros_like(block))
        outgoing[k] = block
        gram[...] += lax.dot_general(
            block, block, (((0,), (0,)), ((), ())), preferred_element_type=F32
        )

    last = leaves - 1

    @pl.loop(0, early)
    def _(k):
        prepare(k)
        copy_to(k).start()

    @pl.loop(early, leaves)
    def _(k):
        prepare(k)

    keep = pltpu.make_async_copy(outgoing.at[last], arrived.at[me], self_sem)
    keep.start()
    group_buf[my_group] = fold_gram(gram[...], snapshots)
    leaf_buf[me] = all_sum("group", groups, group_buf, group_send, group_recv)
    total = all_sum("leaf", leaves, leaf_buf, leaf_send, leaf_recv)

    @pl.loop(early, last)
    def _(k):
        copy_to(k).start()

    upper, inverse = factor_and_inverse(total / rows_all)
    factor_out[...] = upper
    inverse_out[...] = inverse

    keep.wait()

    @pl.loop(1, leaves)
    def _(step):
        copy_from(lax.rem(me + step, leaves)).wait_recv()

    @pl.loop(0, last)
    def _(k):
        copy_to(k).wait_send()


def exchange(tiles, routes, counts, leaves, groups, half, snapshots, rows_all):
    edge = tiles.shape[1]
    slots = tiles.shape[0]
    rows, cols = half * half, half * snapshots
    tables = filter_tables(edge, snapshots)
    vmem = pl.BlockSpec(memory_space=pltpu.VMEM)
    smem = pl.BlockSpec(memory_space=pltpu.SMEM)
    hbm = pl.BlockSpec(memory_space=pl.ANY)
    return pl.pallas_call(
        functools.partial(exchange_kernel, leaves, groups, snapshots, rows_all, 6),
        name="filter_exchange",
        out_shape=(
            jax.ShapeDtypeStruct((leaves, rows, cols), BF16),
            jax.ShapeDtypeStruct((snapshots, 128), F32),
            jax.ShapeDtypeStruct((snapshots, 128), F32),
        ),
        in_specs=[hbm, smem, smem, vmem, vmem, vmem],
        out_specs=(hbm, vmem, vmem),
        scratch_shapes=[
            pltpu.VMEM((slots, edge, edge, edge * snapshots), BF16),
            pltpu.VMEM((leaves, rows, cols), BF16),
            pltpu.VMEM((cols, cols), F32),
            pltpu.VMEM((groups, snapshots, 128), F32),
            pltpu.VMEM((leaves, snapshots, 128), F32),
            pltpu.SemaphoreType.DMA((slots,)),
            pltpu.SemaphoreType.DMA,
            pltpu.SemaphoreType.DMA((leaves,)),
            pltpu.SemaphoreType.DMA((leaves,)),
            pltpu.SemaphoreType.DMA((groups,)),
            pltpu.SemaphoreType.DMA((groups,)),
            pltpu.SemaphoreType.DMA((leaves,)),
            pltpu.SemaphoreType.DMA((leaves,)),
        ],
        compiler_params=pltpu.CompilerParams(
            collective_id=0, has_side_effects=True, vmem_limit_bytes=40 << 20
        ),
    )(tiles, routes, counts, *[jnp.asarray(t) for t in tables])


def apply_kernel(snapshots, blocks, factor, inverse, factor_out, modes, parts):
    @pl.when(pl.program_id(0) == 0)
    def _():
        factor_out[...] = factor[:, :snapshots]
        size = parts.shape[1]
        wide = jnp.concatenate([inverse[...]] * (size // 128), axis=1)
        tall = jnp.concatenate([wide] * (size // snapshots), axis=0)
        rows = lax.broadcasted_iota(jnp.int32, tall.shape, 0) // snapshots
        cols = lax.broadcasted_iota(jnp.int32, tall.shape, 1) // snapshots
        rest = jnp.where(rows == cols, tall, 0.0)
        for p in range(3):
            piece = rest.astype(BF16)
            parts[p] = piece
            rest = rest - piece.astype(F32)

    for b in range(blocks.shape[0]):
        block = blocks[b]
        modes[b] = dot(block, parts[2]) + dot(block, parts[1]) + dot(block, parts[0])


def apply_inverse(blocks, factor, inverse, per_step):
    count, rows, cols = blocks.shape
    snapshots = factor.shape[0]
    whole = lambda shape: pl.BlockSpec(shape, lambda i: (0,) * len(shape))
    step = pl.BlockSpec((per_step, rows, cols), lambda i: (i, 0, 0))
    return pl.pallas_call(
        functools.partial(apply_kernel, snapshots),
        name="apply_inverse",
        out_shape=(
            jax.ShapeDtypeStruct((snapshots, snapshots), F32),
            jax.ShapeDtypeStruct((count, rows, cols), F32),
        ),
        grid=(count // per_step,),
        in_specs=[step, whole(factor.shape), whole(inverse.shape)],
        out_specs=(whole((snapshots, snapshots)), step),
        scratch_shapes=[pltpu.VMEM((3, cols, cols), BF16)],
    )(blocks, factor, inverse)


def shards(tile_fields, routes, counts):
    leaves = lax.axis_size("leaf")
    groups = lax.axis_size("group")
    slots, edge = tile_fields.shape[:2]
    snapshots = tile_fields.shape[3] // edge
    half = edge // 2
    rows_all = half**3 * slots * leaves * groups
    arrived, factor, inverse = exchange(
        tile_fields, routes, counts, leaves, groups, half, snapshots, float(rows_all)
    )
    return apply_inverse(arrived, factor, inverse, 2)


def solution(mesh):
    return jax.shard_map(
        shards,
        mesh=mesh,
        in_specs=(
            P(("leaf", "group"), None, None, None),
            P(("leaf", "group"), None),
            P(("leaf", "group")),
        ),
        out_specs=(P(), P(("leaf", "group"), None, None)),
        check_vma=False,
    )
```

```python
import functools

import jax
import jax.numpy as jnp
import ml_dtypes
import numpy as np
from jax import lax
from jax.experimental import pallas as pl
from jax.experimental.pallas import tpu as pltpu
from jax.sharding import PartitionSpec as P

MESH = pl.DeviceIdType.MESH
F32 = jnp.float32
BF16 = jnp.bfloat16


def smoother(length):
    half_edge = length // 2
    row_index = np.arange(half_edge)[:, None]
    col_index = np.arange(length)[None, :]
    offset = (col_index - 2 * row_index).astype(np.float32)
    tap_offsets = np.arange(-4, 5).astype(np.float32)
    normalizer = np.sum(np.exp(-tap_offsets * tap_offsets / np.float32(4.5)), dtype=np.float32)
    taps = np.exp(-offset * offset / np.float32(4.5)) / normalizer
    weights = np.where(np.abs(offset) <= 4.0, taps, np.float32(0.0))
    return weights.astype(ml_dtypes.bfloat16).astype(np.float32)


def filter_tables(edge, snapshots):
    weights = smoother(edge)
    half = edge // 2
    table_x = np.kron(weights, np.eye(half, dtype=np.float32))
    table_y = np.stack(
        [np.kron(np.eye(half, dtype=np.float32), weights[:, h * half : (h + 1) * half]) for h in range(2)]
    )
    table_z = np.kron(weights.T, np.eye(snapshots, dtype=np.float32))
    as_bf16 = lambda a: a.astype(ml_dtypes.bfloat16)
    return as_bf16(table_x), as_bf16(table_y), as_bf16(table_z)


def dot(a, b):
    return jnp.dot(a, b, preferred_element_type=F32)


def filter_tile(tile, table_x, table_y, table_z):
    edge = tile.shape[0]
    half = edge // 2
    width = tile.shape[2]
    second = None
    for h in range(2):
        rows = tile[:, h * half : (h + 1) * half, :].reshape(edge * half, width)
        first = dot(table_x[...], rows).astype(BF16)
        term = dot(table_y[h], first)
        second = term if second is None else second + term
    return dot(second.astype(BF16), table_z[...]).astype(BF16)


def fold_gram(gram, snapshots):
    size = gram.shape[0]
    rows = lax.broadcasted_iota(jnp.int32, gram.shape, 0) // snapshots
    cols = lax.broadcasted_iota(jnp.int32, gram.shape, 1) // snapshots
    kept = jnp.where(rows == cols, gram, 0.0)
    strip = jnp.sum(kept.reshape(size // snapshots, snapshots, size), axis=0)
    folded = strip[:, :128]
    for start in range(128, size, 128):
        folded = folded + strip[:, start : start + 128]
    shift = 64
    while shift >= snapshots:
        folded = folded + pltpu.roll(folded, shift, axis=1)
        shift //= 2
    return folded


def factor_and_inverse(gram):
    order = gram.shape[0]
    rows = lax.broadcasted_iota(jnp.int32, gram.shape, 0)
    cols = lax.rem(lax.broadcasted_iota(jnp.int32, gram.shape, 1), order)
    rest = gram
    upper = jnp.zeros_like(gram)
    columns = []
    pivots = []
    for r in range(order):
        pivot = jnp.sqrt(rest[r : r + 1, r : r + 1])
        row = jnp.where(cols[:1] >= r, rest[r : r + 1, :] / pivot, 0.0)
        column = jnp.where(rows[:, :1] >= r, rest[:, r : r + 1] / pivot, 0.0)
        upper = jnp.where(rows == r, row, upper)
        columns.append(column)
        pivots.append(pivot)
        rest = rest - column * row
    inverse = jnp.zeros_like(gram)
    for r in range(order - 1, -1, -1):
        beyond = jnp.where(rows[:, :1] > r, columns[r], 0.0)
        unit = jnp.where(cols[:1] == r, 1.0, 0.0)
        row = (unit - jnp.sum(beyond * inverse, axis=0, keepdims=True)) / pivots[r]
        inverse = jnp.where(rows == r, row, inverse)
    return upper, inverse


class Sum:
    def __init__(self, axis, peers, buffer, send_sems, recv_sems):
        self.axis, self.peers, self.buffer = axis, peers, buffer
        self.send_sems, self.recv_sems = send_sems, recv_sems
        self.me = lax.axis_index(axis)

    def copy(self, peer, place):
        return pltpu.make_async_remote_copy(
            src_ref=self.buffer.at[self.me],
            dst_ref=self.buffer.at[place],
            send_sem=self.send_sems.at[peer],
            recv_sem=self.recv_sems.at[place],
            device_id={self.axis: peer},
            device_id_type=MESH,
        )

    def start(self, term):
        self.buffer[self.me] = term

        @pl.loop(1, self.peers)
        def _(step):
            self.copy(lax.rem(self.me + step, self.peers), self.me).start()

    def finish(self):
        @pl.loop(1, self.peers)
        def _(step):
            peer = lax.rem(self.me + step, self.peers)
            self.copy(peer, peer).wait_recv()

        total = self.buffer[0]
        for p in range(1, self.peers):
            total = total + self.buffer[p]

        @pl.loop(1, self.peers)
        def _(step):
            self.copy(lax.rem(self.me + step, self.peers), self.me).wait_send()

        return total


def split_inverse(inverse, parts, snapshots):
    size = parts.shape[1]
    wide = jnp.concatenate([inverse] * (size // 128), axis=1)
    tall = jnp.concatenate([wide] * (size // snapshots), axis=0)
    rows = lax.broadcasted_iota(jnp.int32, tall.shape, 0) // snapshots
    cols = lax.broadcasted_iota(jnp.int32, tall.shape, 1) // snapshots
    rest = jnp.where(rows == cols, tall, 0.0)
    for p in range(3):
        piece = rest.astype(BF16)
        parts[(2 - p) * size : (3 - p) * size, :] = piece
        rest = rest - piece.astype(F32)


def exchange_kernel(
    leaves, groups, snapshots, rows_all,
    tiles, routes_hbm, counts, table_x_hbm, table_y_hbm, table_z_hbm,
    factor_out, modes,
    routes, local, table_x, table_y, table_z, filtered, outgoing, relay, arrived, gram, parts, group_buf, leaf_buf,
    load_sems, table_sems, send_sems, recv_sems, relay_send, relay_recv,
    group_send, group_recv, leaf_send, leaf_recv,
):
    slots = tiles.shape[0]
    me = lax.axis_index("leaf")
    my_group = lax.axis_index("group")
    chips = leaves // 2
    far = chips // 2
    chip, core = me // 2, lax.rem(me, 2)

    loads = [
        pltpu.make_async_copy(src, dst, table_sems.at[n])
        for n, (src, dst) in enumerate(
            (
                (routes_hbm, routes),
                (table_x_hbm, table_x),
                (table_y_hbm, table_y),
                (table_z_hbm, table_z),
            )
        )
    ]
    loads += [pltpu.make_async_copy(tiles.at[t], local.at[t], load_sems.at[t]) for t in range(slots)]
    for copy in loads:
        copy.start()

    barrier = pltpu.get_barrier_semaphore()

    @pl.loop(1, leaves)
    def _(step):
        pl.semaphore_signal(
            barrier, inc=1, device_id={"leaf": lax.rem(me + step, leaves)}, device_id_type=MESH
        )

    @pl.loop(1, groups)
    def _(step):
        pl.semaphore_signal(
            barrier, inc=1, device_id={"group": lax.rem(my_group + step, groups)}, device_id_type=MESH
        )

    gram[...] = jnp.zeros_like(gram)
    for copy in loads:
        copy.wait()
    pl.semaphore_wait(barrier, leaves + groups - 2)

    def leaf_at(turn, flip):
        return lax.rem(chip + turn + chips, chips) * 2 + lax.rem(core + flip, 2)

    def dest_of(k):
        place = k + 2
        distance = far - place // 4
        m = lax.rem(place, 4)
        ahead = jnp.where(lax.rem(m, 2) == 0, distance, -distance)
        flip = jnp.where((m == 1) | (m == 2), 1, 0)
        half_way = k < 2
        near = k >= leaves - 2
        ahead = jnp.where(half_way, far, jnp.where(near, 0, ahead))
        flip = jnp.where(half_way, k, jnp.where(near, leaves - 1 - k, flip))
        return leaf_at(ahead, flip)

    def send(src, sender, sems, k, dest):
        return pltpu.make_async_remote_copy(
            src_ref=src,
            dst_ref=arrived.at[sender],
            send_sem=sems.at[k],
            recv_sem=recv_sems.at[sender],
            device_id={"leaf": dest},
            device_id_type=MESH,
        )

    def direct(k):
        return send(outgoing.at[k], me, send_sems, k, dest_of(k))

    def first_hop(k):
        return pltpu.make_async_remote_copy(
            src_ref=outgoing.at[k],
            dst_ref=relay.at[k],
            send_sem=send_sems.at[k],
            recv_sem=relay_recv.at[k],
            device_id={"leaf": leaf_at(1 - 2 * k, 0)},
            device_id_type=MESH,
        )

    def last_hops(k):
        sender = leaf_at(2 * k - 1, 0)
        return send(relay.at[k], sender, relay_send, k, leaf_at((far - 1) * (1 - 2 * k), k))

    count = counts[0]

    def slot_for(dest):
        slot = jnp.int32(0)
        found = jnp.int32(0)
        for t in range(slots):
            hit = jnp.where((routes[0, t] == dest) & (t < count), 1, 0)
            slot = slot + hit * t
            found = found + hit
        return slot, found > 0

    def prepare(k, block_of):
        slot, found = slot_for(dest_of(k))
        block = block_of(slot)
        outgoing[k] = jnp.where(found, block, jnp.zeros_like(block))

    early = 4
    for k in range(early):
        prepare(k, lambda slot: filter_tile(local[slot], table_x, table_y, table_z))
        (first_hop(k) if k < 2 else direct(k)).start()

    @pl.loop(0, slots)
    def _(t):
        block = filter_tile(local[t], table_x, table_y, table_z)
        block = jnp.where(t < count, block, jnp.zeros_like(block))
        filtered[t] = block
        gram[...] += lax.dot_general(
            block, block, (((0,), (0,)), ((), ())), preferred_element_type=F32
        )

    middle = 10

    @pl.loop(early, middle)
    def _(k):
        prepare(k, lambda slot: filtered[slot])
        direct(k).start()

    for k in range(2):
        first_hop(k).wait_recv()
        last_hops(k).start()

    group_sum = Sum("group", groups, group_buf, group_send, group_recv)
    group_sum.start(fold_gram(gram[...], snapshots))
    group_total = group_sum.finish()
    leaf_sum = Sum("leaf", leaves, leaf_buf, leaf_send, leaf_recv)
    leaf_sum.start(group_total)

    last = leaves - 1

    @pl.loop(middle, last)
    def _(k):
        prepare(k, lambda slot: filtered[slot])
        direct(k).start()

    prepare(last, lambda slot: filtered[slot])
    total = leaf_sum.finish()
    upper, inverse = factor_and_inverse(total / rows_all)
    factor_out[...] = upper[:, :snapshots]
    split_inverse(inverse, parts, snapshots)

    def apply(block):
        return dot(jnp.concatenate([block] * 3, axis=1), parts[...])

    modes[me] = apply(outgoing[last])

    @pl.loop(0, last)
    def _(n):
        k = jnp.where(n == 0, last - 1, jnp.where(n < 5, n + 1, jnp.where(n < 7, n - 5, n - 1)))
        source = dest_of(k)
        send(outgoing.at[0], source, send_sems, 0, source).wait_recv()
        modes[source] = apply(arrived[source])

    for k in range(2):
        first_hop(k).wait_send()
        last_hops(k).wait_send()

    @pl.loop(2, last)
    def _(k):
        direct(k).wait_send()


def exchange(tiles, routes, counts, leaves, groups, half, snapshots, rows_all):
    edge = tiles.shape[1]
    slots = tiles.shape[0]
    rows, cols = half * half, half * snapshots
    tables = filter_tables(edge, snapshots)
    vmem = pl.BlockSpec(memory_space=pltpu.VMEM)
    hbm = pl.BlockSpec(memory_space=pltpu.HBM)
    keep = lambda a: pltpu.with_memory_space_constraint(a, pltpu.HBM)
    return pl.pallas_call(
        functools.partial(exchange_kernel, leaves, groups, snapshots, rows_all),
        name="filter_exchange",
        out_shape=(
            jax.ShapeDtypeStruct((snapshots, snapshots), F32),
            jax.ShapeDtypeStruct((leaves, rows, cols), F32),
        ),
        in_specs=[hbm, hbm, pl.BlockSpec(memory_space=pltpu.SMEM), hbm, hbm, hbm],
        out_specs=(vmem, vmem),
        scratch_shapes=[
            pltpu.SMEM(routes.shape, jnp.int32),
            pltpu.VMEM((slots, edge, edge, edge * snapshots), BF16),
            *[pltpu.VMEM(t.shape, BF16) for t in tables],
            pltpu.VMEM((slots, rows, cols), BF16),
            pltpu.VMEM((leaves, rows, cols), BF16),
            pltpu.VMEM((2, rows, cols), BF16),
            pltpu.VMEM((leaves, rows, cols), BF16),
            pltpu.VMEM((cols, cols), F32),
            pltpu.VMEM((3 * cols, cols), BF16),
            pltpu.VMEM((groups, snapshots, 128), F32),
            pltpu.VMEM((leaves, snapshots, 128), F32),
            pltpu.SemaphoreType.DMA((slots,)),
            pltpu.SemaphoreType.DMA((4,)),
            pltpu.SemaphoreType.DMA((leaves,)),
            pltpu.SemaphoreType.DMA((leaves,)),
            pltpu.SemaphoreType.DMA((2,)),
            pltpu.SemaphoreType.DMA((2,)),
            pltpu.SemaphoreType.DMA((groups,)),
            pltpu.SemaphoreType.DMA((groups,)),
            pltpu.SemaphoreType.DMA((leaves,)),
            pltpu.SemaphoreType.DMA((leaves,)),
        ],
        compiler_params=pltpu.CompilerParams(
            collective_id=0, has_side_effects=True, vmem_limit_bytes=40 << 20
        ),
    )(keep(tiles), keep(routes), counts, *[keep(jnp.asarray(t)) for t in tables])


def shards(tile_fields, routes, counts):
    leaves = lax.axis_size("leaf")
    groups = lax.axis_size("group")
    slots, edge = tile_fields.shape[:2]
    snapshots = tile_fields.shape[3] // edge
    half = edge // 2
    rows_all = half**3 * slots * leaves * groups
    return exchange(
        tile_fields, routes, counts, leaves, groups, half, snapshots, float(rows_all)
    )


def solution(mesh):
    return jax.shard_map(
        shards,
        mesh=mesh,
        in_specs=(
            P(("leaf", "group"), None, None, None),
            P(("leaf", "group"), None),
            P(("leaf", "group")),
        ),
        out_specs=(P(), P(("leaf", "group"), None, None)),
        check_vma=False,
    )
```

```python
import functools

import jax
import jax.numpy as jnp
import ml_dtypes
import numpy as np
from jax import lax
from jax.experimental import pallas as pl
from jax.experimental.pallas import tpu as pltpu
from jax.sharding import PartitionSpec as P

MESH = pl.DeviceIdType.MESH
F32 = jnp.float32
BF16 = jnp.bfloat16


def smoother(length):
    half_edge = length // 2
    row_index = np.arange(half_edge)[:, None]
    col_index = np.arange(length)[None, :]
    offset = (col_index - 2 * row_index).astype(np.float32)
    tap_offsets = np.arange(-4, 5).astype(np.float32)
    normalizer = np.sum(np.exp(-tap_offsets * tap_offsets / np.float32(4.5)), dtype=np.float32)
    taps = np.exp(-offset * offset / np.float32(4.5)) / normalizer
    weights = np.where(np.abs(offset) <= 4.0, taps, np.float32(0.0))
    return weights.astype(ml_dtypes.bfloat16).astype(np.float32)


def filter_tables(edge, snapshots):
    weights = smoother(edge)
    half = edge // 2
    table_x = np.kron(weights, np.eye(half, dtype=np.float32))
    table_y = np.stack(
        [np.kron(np.eye(half, dtype=np.float32), weights[:, h * half : (h + 1) * half]) for h in range(2)]
    )
    table_z = np.kron(weights.T, np.eye(snapshots, dtype=np.float32))
    as_bf16 = lambda a: a.astype(ml_dtypes.bfloat16)
    return as_bf16(table_x), as_bf16(table_y), as_bf16(table_z)


def dot(a, b):
    return jnp.dot(a, b, preferred_element_type=F32)


def filter_tile(tile, table_x, table_y, table_z):
    edge = tile.shape[0]
    half = edge // 2
    width = tile.shape[2]
    second = None
    for h in range(2):
        rows = tile[:, h * half : (h + 1) * half, :].reshape(edge * half, width)
        first = dot(table_x[...], rows).astype(BF16)
        term = dot(table_y[h], first)
        second = term if second is None else second + term
    return dot(second.astype(BF16), table_z[...]).astype(BF16)


def fold_gram(gram, snapshots):
    size = gram.shape[0]
    rows = lax.broadcasted_iota(jnp.int32, gram.shape, 0) // snapshots
    cols = lax.broadcasted_iota(jnp.int32, gram.shape, 1) // snapshots
    kept = jnp.where(rows == cols, gram, 0.0)
    strip = jnp.sum(kept.reshape(size // snapshots, snapshots, size), axis=0)
    folded = strip[:, :128]
    for start in range(128, size, 128):
        folded = folded + strip[:, start : start + 128]
    shift = 64
    while shift >= snapshots:
        folded = folded + pltpu.roll(folded, shift, axis=1)
        shift //= 2
    return folded


def factor_and_inverse(gram):
    order = gram.shape[0]
    rows = lax.broadcasted_iota(jnp.int32, gram.shape, 0)
    cols = lax.rem(lax.broadcasted_iota(jnp.int32, gram.shape, 1), order)
    rest = gram
    upper = jnp.zeros_like(gram)
    columns = []
    pivots = []
    for r in range(order):
        pivot = jnp.sqrt(rest[r : r + 1, r : r + 1])
        row = jnp.where(cols[:1] >= r, rest[r : r + 1, :] / pivot, 0.0)
        column = jnp.where(rows[:, :1] >= r, rest[:, r : r + 1] / pivot, 0.0)
        upper = jnp.where(rows == r, row, upper)
        columns.append(column)
        pivots.append(pivot)
        rest = rest - column * row
    inverse = jnp.zeros_like(gram)
    for r in range(order - 1, -1, -1):
        beyond = jnp.where(rows[:, :1] > r, columns[r], 0.0)
        unit = jnp.where(cols[:1] == r, 1.0, 0.0)
        row = (unit - jnp.sum(beyond * inverse, axis=0, keepdims=True)) / pivots[r]
        inverse = jnp.where(rows == r, row, inverse)
    return upper, inverse


class Sum:
    def __init__(self, axis, peers, buffer, send_sems, recv_sems):
        self.axis, self.peers, self.buffer = axis, peers, buffer
        self.send_sems, self.recv_sems = send_sems, recv_sems
        self.me = lax.axis_index(axis)

    def copy(self, peer, place):
        return pltpu.make_async_remote_copy(
            src_ref=self.buffer.at[self.me],
            dst_ref=self.buffer.at[place],
            send_sem=self.send_sems.at[peer],
            recv_sem=self.recv_sems.at[place],
            device_id={self.axis: peer},
            device_id_type=MESH,
        )

    def start(self, term):
        self.buffer[self.me] = term

        @pl.loop(1, self.peers)
        def _(step):
            self.copy(lax.rem(self.me + step, self.peers), self.me).start()

    def finish(self):
        @pl.loop(1, self.peers)
        def _(step):
            peer = lax.rem(self.me + step, self.peers)
            self.copy(peer, peer).wait_recv()

        total = self.buffer[0]
        for p in range(1, self.peers):
            total = total + self.buffer[p]

        @pl.loop(1, self.peers)
        def _(step):
            self.copy(lax.rem(self.me + step, self.peers), self.me).wait_send()

        return total


def split_inverse(inverse, parts, snapshots):
    size = parts.shape[1]
    wide = jnp.concatenate([inverse] * (size // 128), axis=1)
    tall = jnp.concatenate([wide] * (size // snapshots), axis=0)
    rows = lax.broadcasted_iota(jnp.int32, tall.shape, 0) // snapshots
    cols = lax.broadcasted_iota(jnp.int32, tall.shape, 1) // snapshots
    rest = jnp.where(rows == cols, tall, 0.0)
    for p in range(3):
        piece = rest.astype(BF16)
        parts[(2 - p) * size : (3 - p) * size, :] = piece
        rest = rest - piece.astype(F32)


def exchange_kernel(
    leaves, groups, snapshots, rows_all,
    tiles, routes_hbm, counts, table_x_hbm, table_y_hbm, table_z_hbm,
    factor_out, modes,
    routes, local, table_x, table_y, table_z, filtered, outgoing, relay, arrived, gram, parts, group_buf, leaf_buf,
    load_sems, table_sems, send_sems, recv_sems, relay_send, relay_recv,
    group_send, group_recv, leaf_send, leaf_recv,
):
    slots = tiles.shape[0]
    me = lax.axis_index("leaf")
    my_group = lax.axis_index("group")
    chips = leaves // 2
    far = chips // 2
    chip, core = me // 2, lax.rem(me, 2)

    loads = [
        pltpu.make_async_copy(src, dst, table_sems.at[n])
        for n, (src, dst) in enumerate(
            (
                (routes_hbm, routes),
                (table_x_hbm, table_x),
                (table_y_hbm, table_y),
                (table_z_hbm, table_z),
            )
        )
    ]
    loads += [pltpu.make_async_copy(tiles.at[t], local.at[t], load_sems.at[t]) for t in range(slots)]
    for copy in loads:
        copy.start()

    barrier = pltpu.get_barrier_semaphore()

    @pl.loop(1, leaves)
    def _(step):
        pl.semaphore_signal(
            barrier, inc=1, device_id={"leaf": lax.rem(me + step, leaves)}, device_id_type=MESH
        )

    @pl.loop(1, groups)
    def _(step):
        pl.semaphore_signal(
            barrier, inc=1, device_id={"group": lax.rem(my_group + step, groups)}, device_id_type=MESH
        )

    gram[...] = jnp.zeros_like(gram)
    for copy in loads:
        copy.wait()
    pl.semaphore_wait(barrier, leaves + groups - 2)

    def leaf_at(turn, flip):
        return lax.rem(chip + turn + chips, chips) * 2 + lax.rem(core + flip, 2)

    def dest_of(k):
        place = k + 2
        distance = far - place // 4
        m = lax.rem(place, 4)
        ahead = jnp.where(lax.rem(m, 2) == 0, distance, -distance)
        flip = jnp.where((m == 1) | (m == 2), 1, 0)
        half_way = k < 2
        near = k >= leaves - 2
        ahead = jnp.where(half_way, far, jnp.where(near, 0, ahead))
        flip = jnp.where(half_way, k, jnp.where(near, leaves - 1 - k, flip))
        return leaf_at(ahead, flip)

    def send(src, sender, sems, k, dest):
        return pltpu.make_async_remote_copy(
            src_ref=src,
            dst_ref=arrived.at[sender],
            send_sem=sems.at[k],
            recv_sem=recv_sems.at[sender],
            device_id={"leaf": dest},
            device_id_type=MESH,
        )

    def direct(k):
        return send(outgoing.at[k], me, send_sems, k, dest_of(k))

    def first_hop(k):
        return pltpu.make_async_remote_copy(
            src_ref=outgoing.at[k],
            dst_ref=relay.at[k],
            send_sem=send_sems.at[k],
            recv_sem=relay_recv.at[k],
            device_id={"leaf": leaf_at(1 - 2 * k, 0)},
            device_id_type=MESH,
        )

    def last_hops(k):
        sender = leaf_at(2 * k - 1, 0)
        return send(relay.at[k], sender, relay_send, k, leaf_at((far - 1) * (1 - 2 * k), k))

    count = counts[0]

    def slot_for(dest):
        slot = jnp.int32(0)
        found = jnp.int32(0)
        for t in range(slots):
            hit = jnp.where((routes[0, t] == dest) & (t < count), 1, 0)
            slot = slot + hit * t
            found = found + hit
        return slot, found > 0

    def prepare(k, block_of):
        slot, found = slot_for(dest_of(k))
        block = block_of(slot)
        outgoing[k] = jnp.where(found, block, jnp.zeros_like(block))

    early = 4

    @pl.loop(0, early)
    def _(k):
        prepare(k, lambda slot: filter_tile(local[slot], table_x, table_y, table_z))

        @pl.when(k < 2)
        def _():
            first_hop(k).start()

        @pl.when(k >= 2)
        def _():
            direct(k).start()

    @pl.loop(0, slots)
    def _(t):
        block = filter_tile(local[t], table_x, table_y, table_z)
        block = jnp.where(t < count, block, jnp.zeros_like(block))
        filtered[t] = block
        gram[...] += lax.dot_general(
            block, block, (((0,), (0,)), ((), ())), preferred_element_type=F32
        )

    leaf_sum = Sum("leaf", leaves, leaf_buf, leaf_send, leaf_recv)
    leaf_sum.start(fold_gram(gram[...], snapshots))
    last = leaves - 1
    near = last - 5

    def send_blocks(first, end):
        @pl.loop(first, end)
        def _(k):
            prepare(k, lambda slot: filtered[slot])
            direct(k).start()

    send_blocks(early, near)
    for k in range(2):
        first_hop(k).wait_recv()
        last_hops(k).start()
    send_blocks(near, last)
    prepare(last, lambda slot: filtered[slot])

    group_sum = Sum("group", groups, group_buf, group_send, group_recv)
    group_sum.start(leaf_sum.finish())
    upper, inverse = factor_and_inverse(group_sum.finish() / rows_all)
    factor_out[...] = upper[:, :snapshots]
    split_inverse(inverse, parts, snapshots)

    def apply(block):
        return dot(jnp.concatenate([block] * 3, axis=1), parts[...])

    modes[me] = apply(outgoing[last])

    @pl.loop(0, last)
    def _(n):
        k = jnp.where(n < near - 1, n + 1, jnp.where(n < near + 1, n - near + 1, n - 1))
        k = jnp.where(n == 0, last - 1, k)
        source = dest_of(k)
        send(outgoing.at[0], source, send_sems, 0, source).wait_recv()
        modes[source] = apply(arrived[source])

    for k in range(2):
        first_hop(k).wait_send()
        last_hops(k).wait_send()

    @pl.loop(2, last)
    def _(k):
        direct(k).wait_send()


def exchange(tiles, routes, counts, leaves, groups, half, snapshots, rows_all):
    edge = tiles.shape[1]
    slots = tiles.shape[0]
    rows, cols = half * half, half * snapshots
    tables = filter_tables(edge, snapshots)
    vmem = pl.BlockSpec(memory_space=pltpu.VMEM)
    hbm = pl.BlockSpec(memory_space=pltpu.HBM)
    keep = lambda a: pltpu.with_memory_space_constraint(a, pltpu.HBM)
    return pl.pallas_call(
        functools.partial(exchange_kernel, leaves, groups, snapshots, rows_all),
        name="filter_exchange",
        out_shape=(
            jax.ShapeDtypeStruct((snapshots, snapshots), F32),
            jax.ShapeDtypeStruct((leaves, rows, cols), F32),
        ),
        in_specs=[hbm, hbm, pl.BlockSpec(memory_space=pltpu.SMEM), hbm, hbm, hbm],
        out_specs=(vmem, vmem),
        scratch_shapes=[
            pltpu.SMEM(routes.shape, jnp.int32),
            pltpu.VMEM((slots, edge, edge, edge * snapshots), BF16),
            *[pltpu.VMEM(t.shape, BF16) for t in tables],
            pltpu.VMEM((slots, rows, cols), BF16),
            pltpu.VMEM((leaves, rows, cols), BF16),
            pltpu.VMEM((2, rows, cols), BF16),
            pltpu.VMEM((leaves, rows, cols), BF16),
            pltpu.VMEM((cols, cols), F32),
            pltpu.VMEM((3 * cols, cols), BF16),
            pltpu.VMEM((groups, snapshots, 128), F32),
            pltpu.VMEM((leaves, snapshots, 128), F32),
            pltpu.SemaphoreType.DMA((slots,)),
            pltpu.SemaphoreType.DMA((4,)),
            pltpu.SemaphoreType.DMA((leaves,)),
            pltpu.SemaphoreType.DMA((leaves,)),
            pltpu.SemaphoreType.DMA((2,)),
            pltpu.SemaphoreType.DMA((2,)),
            pltpu.SemaphoreType.DMA((groups,)),
            pltpu.SemaphoreType.DMA((groups,)),
            pltpu.SemaphoreType.DMA((leaves,)),
            pltpu.SemaphoreType.DMA((leaves,)),
        ],
        compiler_params=pltpu.CompilerParams(
            collective_id=0, has_side_effects=True, vmem_limit_bytes=40 << 20
        ),
    )(keep(tiles), keep(routes), counts, *[keep(jnp.asarray(t)) for t in tables])


def store_kernel(factor, modes, factor_out, modes_out, sems):
    pieces = sems.shape[0] - 1
    size = modes.shape[0] // pieces
    copies = [
        pltpu.make_async_copy(
            modes.at[pl.ds(p * size, size)], modes_out.at[pl.ds(p * size, size)], sems.at[p]
        )
        for p in range(pieces)
    ]
    copies.append(pltpu.make_async_copy(factor, factor_out, sems.at[pieces]))
    for copy in copies:
        copy.start()
    for copy in copies:
        copy.wait()


def store(factor, modes):
    vmem = pl.BlockSpec(memory_space=pltpu.VMEM)
    hbm = pl.BlockSpec(memory_space=pltpu.HBM)
    return pl.pallas_call(
        store_kernel,
        name="store",
        out_shape=(
            jax.ShapeDtypeStruct(factor.shape, factor.dtype),
            jax.ShapeDtypeStruct(modes.shape, modes.dtype),
        ),
        in_specs=[vmem, vmem],
        out_specs=(hbm, hbm),
        scratch_shapes=[pltpu.SemaphoreType.DMA((5,))],
        compiler_params=pltpu.CompilerParams(vmem_limit_bytes=16 << 20),
    )(factor, modes)


def shards(tile_fields, routes, counts):
    leaves = lax.axis_size("leaf")
    groups = lax.axis_size("group")
    slots, edge = tile_fields.shape[:2]
    snapshots = tile_fields.shape[3] // edge
    half = edge // 2
    rows_all = half**3 * slots * leaves * groups
    factor, modes = exchange(
        tile_fields, routes, counts, leaves, groups, half, snapshots, float(rows_all)
    )
    return store(factor, modes)


def solution(mesh):
    return jax.shard_map(
        shards,
        mesh=mesh,
        in_specs=(
            P(("leaf", "group"), None, None, None),
            P(("leaf", "group"), None),
            P(("leaf", "group")),
        ),
        out_specs=(P(), P(("leaf", "group"), None, None)),
        check_vma=False,
    )
```
